32 devices in a mesh: dp: 4 (over x, core), context: 8 (over z, y).
Axes of the slice: x: 2, y: 2, z: 4, core: 2. Of those that a mesh axis runs over, the one named last changes fastest.
Arguments:
- tokens: bfloat16 [4, 2048, 2048], P('dp', 'context'), may hold values from -6 to 6
- weight: bfloat16 [2048, 2048], P('context'), may hold values from -0.125 to 0.125
- gate: bfloat16 [4, 2048, 2048], P('dp', 'context'), may hold values from -6 to 6
- skip: float32 [2048], replicated, may hold values from 0.1 to 1.9
- first_factor: bfloat16 [16, 128, 128], P('context'), may hold values from -0.5 to 0.5
- second_factor: bfloat16 [128, 16, 16], P('context'), may hold values from -1.5 to 1.5
- kernel: bfloat16 [16, 128, 2048], P(None, 'context'), may hold values from -6 to 6
- third_factor: bfloat16 [128, 16, 16], P('context'), may hold values from -1.5 to 1.5
- fourth_factor: bfloat16 [16, 128, 128], P('context'), may hold values from -0.5 to 0.5
- cotangent: bfloat16 [4, 2048, 2048], P('dp', 'context'), may hold values from -6 to 6
Outputs:
- mixed: bfloat16 [4, 2048, 2048], P('dp', 'context')
- grad_tokens: bfloat16 [4, 2048, 2048], P('dp', 'context')
- grad_gate: bfloat16 [4, 2048, 2048], P('dp', 'context')
- grad_weight: float32 [2048, 2048], P('context')
The draws below stay inside these ranges and needn't reach their ends.
All inputs are finite; a program needn't handle non-finite values.
Results may differ from the reference program's by a relative error of at most 0.019.
Values may be sent and summed in bfloat16 or wider, within the bound.
No kernel may reach another device: no remote copies, remote signals or barrier semaphores. Data moves between devices by JAX's collectives and lax.ppermute only.
A program may use at most 128 MiB of HBM per device.

```python
import jax
import jax.numpy as jnp
from jax import lax

D = 2048
R = 128
TOK_DEV = 256
SEQS = 4
N = 2048
Q = 16
N_CONTEXT = 8


def strengthened(entries, rng, source, target, parts, factor):
    def block_of(dim):
        return (jnp.arange(entries.shape[dim]) // (entries.shape[dim] // parts)).reshape((-1,) + (1,) * (entries.ndim - 1 - dim))

    near = jax.random.permutation(rng, parts)[block_of(target)]
    other_side = (block_of(target) + parts // 2) % parts
    return jnp.where((block_of(source) == near) | (block_of(source) == other_side), factor * entries, entries)


def block_levels(rng, extent, split, least, high):
    loudness, own = 1.0, jax.random.fold_in(rng, 6)
    for dim, shards_of in split:
        draws = jnp.exp(jax.random.uniform(jax.random.fold_in(own, dim), (shards_of,), jnp.float32, least / len(split), high / len(split)))
        loudness = loudness * jnp.repeat(draws, extent[dim] // shards_of).reshape([-1 if axis == dim else 1 for axis in range(len(extent))])
    return loudness


def scatter_about(key, shape, scale, most, shards=(), kind=jnp.bfloat16):
    values = scale * jax.random.normal(key, shape, jnp.float32)
    if shards:
        values = values * block_levels(key, shape, shards, -0.22, 0.18)
    return jnp.clip(values, -most, most).astype(kind)


def noise_with(own_key, extent, spread, limit, cuts, heavy, kind=jnp.bfloat16):
    drawn = spread * jax.random.normal(own_key, extent, jnp.float32)
    if cuts:
        drawn = drawn * block_levels(own_key, extent, cuts, -0.22, 0.18)
    return jnp.clip(strengthened(drawn, jax.random.fold_in(own_key, 3), *heavy), -limit, limit).astype(kind)


def setup_inputs(seed: int = 0) -> dict:
    seeds = jax.random.split(jax.random.key(seed), 11)
    tokens = noise_with(seeds[0], (SEQS, N, D), 1.0, 6.0, ((0, 4), (1, 8)), (1, 2, 8, 2.0))
    weight = scatter_about(seeds[1], (D, D), D ** -0.5, 0.125, ((0, 8),))
    gate = scatter_about(seeds[2], (SEQS, N, D), 1.0, 6.0, ((0, 4), (1, 8)))
    skip = jnp.clip(1.0 + 0.18 * jax.random.normal(seeds[3], (D,), jnp.float32), 0.1, 1.9)
    first_factor = scatter_about(seeds[4], (Q, R, R), R ** -0.5, 0.5, ((0, 8),))
    second_factor = scatter_about(seeds[5], (R, Q, Q), Q ** -0.5, 1.5, ((0, 8),))
    kernel = scatter_about(seeds[6], (Q, R, D), 1.0, 6.0, ((1, 8),))
    third_factor = scatter_about(seeds[7], (R, Q, Q), Q ** -0.5, 1.5, ((0, 8),))
    fourth_factor = scatter_about(seeds[8], (Q, R, R), R ** -0.5, 0.5, ((0, 8),))
    cotangent = scatter_about(seeds[9], (SEQS, N, D), 1.0, 6.0, ((0, 4), (1, 8)))
    return {"tokens": tokens, "weight": weight, "gate": gate, "skip": skip, "first_factor": first_factor, "second_factor": second_factor, "kernel": kernel, "third_factor": third_factor, "fourth_factor": fourth_factor, "cotangent": cotangent}


def widen(value):
    return value.astype(jnp.float32)


def reference(tokens, weight, gate, skip, first_factor, second_factor, kernel, third_factor, fourth_factor, cotangent):
    fac_one = widen(first_factor)
    fac_two = widen(second_factor)
    fac_three = widen(third_factor)
    fac_four = widen(fourth_factor)
    kern = widen(kernel)

    def one_sequence(total, inputs):
        seq_tokens, seq_gate, seq_grad = inputs
        proj = jnp.dot(seq_tokens, weight, preferred_element_type=jnp.float32).astype(jnp.bfloat16)
        proj_blocks = widen(proj).reshape(Q, R, D)
        first_mix = jnp.einsum('qsr,qrc->qsc', fac_one, proj_blocks).astype(jnp.bfloat16)
        second_mix = jnp.einsum('stq,qsc->tsc', fac_two, widen(first_mix))
        filtered = (second_mix * kern).astype(jnp.bfloat16)
        third_mix = jnp.einsum('spt,tsc->psc', fac_three, widen(filtered)).astype(jnp.bfloat16)
        field = jnp.einsum('qrs,qsc->qrc', fac_four, widen(third_mix)).reshape(N, D)
        pre_gate = field + skip * widen(proj)
        gate_vals = widen(seq_gate)
        out_grad = widen(seq_grad)
        mixed = (gate_vals * pre_gate).astype(jnp.bfloat16)
        grad_gate = (out_grad * pre_gate).astype(jnp.bfloat16)
        gated_grad = (out_grad * gate_vals).astype(jnp.bfloat16)
        grad_third = jnp.einsum('qrs,qrc->qsc', fac_four, widen(gated_grad).reshape(Q, R, D)).astype(jnp.bfloat16)
        grad_filtered_in = jnp.einsum('spt,psc->tsc', fac_three, widen(grad_third))
        grad_second = (grad_filtered_in * kern).astype(jnp.bfloat16)
        grad_first = jnp.einsum('stq,tsc->qsc', fac_two, widen(grad_second)).astype(jnp.bfloat16)
        grad_field = jnp.einsum('qsr,qsc->qrc', fac_one, widen(grad_first)).reshape(N, D)
        grad_proj = (grad_field + skip * widen(gated_grad)).astype(jnp.bfloat16)
        grad_tokens = jnp.dot(grad_proj, weight.T, preferred_element_type=jnp.float32).astype(jnp.bfloat16)
        token_runs = seq_tokens.reshape(N_CONTEXT, TOK_DEV, D)
        grad_runs = grad_proj.reshape(N_CONTEXT, TOK_DEV, D)

        def add_run(running, block_pair):
            partial_value = jnp.dot(block_pair[0].T, block_pair[1], preferred_element_type=jnp.float32).astype(jnp.bfloat16)
            return running + widen(partial_value), None

        total, _ = lax.scan(add_run, total, (token_runs, grad_runs))
        return total, (mixed, grad_tokens, grad_gate)

    start_total = jnp.zeros((D, D), jnp.float32)
    grad_weight, outputs = lax.scan(one_sequence, start_total, (tokens, gate, cotangent))
    return outputs[0], outputs[1], outputs[2], grad_weight
```

```python
import jax
import jax.numpy as jnp
from jax import lax
from jax.sharding import PartitionSpec as P


BF16 = jnp.bfloat16
F32 = jnp.float32


def dot(a, b, ca=1, cb=0):
    return lax.dot_general(a, b, (((ca,), (cb,)), ((), ())), preferred_element_type=F32)


def exchange(x, axis, bit):
    n = lax.axis_size(axis)
    return lax.ppermute(x, axis, [(i, i ^ bit) for i in range(n)])


def bits_of(n):
    return [1 << i for i in range(n.bit_length() - 1)]


def gather_blocks(own, axis):
    have = {0: own}
    for bit in reversed(bits_of(lax.axis_size(axis))):
        have.update({m ^ bit: exchange(x, axis, bit) for m, x in list(have.items())})
    return [have[m] for m in range(len(have))]


def reduce_blocks(blocks, axis):
    terms = dict(enumerate(blocks))
    for bit in bits_of(lax.axis_size(axis)):
        last = len(terms) == 2
        got = {m: exchange(terms[m ^ bit], axis, bit) for m in terms if not m & bit}
        summed = {m: terms[m].astype(F32) + got[m].astype(F32) for m in got}
        terms = summed if last else {m: x.astype(BF16) for m, x in summed.items()}
    return terms[0]


def swap_blocks(blocks, axis):
    return [blocks[0]] + [exchange(blocks[m], axis, m) for m in range(1, len(blocks))]


def in_order(blocks, me, axis):
    stack = jnp.stack(blocks)
    return jnp.concatenate(
        [lax.dynamic_index_in_dim(stack, me ^ j, 0, keepdims=False) for j in range(len(blocks))],
        axis=axis,
    )


def columns_of(x, index, count):
    width = x.shape[1] // count
    return lax.dynamic_slice_in_dim(x, index * width, width, axis=1)


def iota(shape, dim):
    return lax.broadcasted_iota(jnp.int32, shape, dim)


def per_device(
    tokens,
    weight,
    gate,
    skip,
    first_factor,
    second_factor,
    kernel,
    third_factor,
    fourth_factor,
    cotangent,
):
    nc, nd = lax.axis_size("context"), lax.axis_size("dp")
    me, lane = lax.axis_index("context"), lax.axis_index("dp")
    own = tokens[0]
    rows, width = own.shape
    q_loc, block, _ = first_factor.shape
    s_loc, q_all, _ = second_factor.shape
    part = q_loc * s_loc
    mid = q_all * s_loc

    row = iota((rows, block), 0)
    source = (me ^ (row // part)) * s_loc + row % s_loc
    pick = (source == iota((rows, block), 1)).astype(BF16)
    of_q = (iota((rows, block), 0) % part) // s_loc

    def diagonal(factor, contract):
        return jnp.concatenate(
            [
                jnp.where(of_q == q, dot(pick, factor[q], 1, contract), 0).astype(BF16)
                for q in range(q_loc)
            ],
            axis=1,
        )

    fourth = diagonal(fourth_factor, 1)
    first = diagonal(first_factor, 0)

    def xor_q(index):
        return (me ^ (index // part)) * q_loc + (index % part) // s_loc

    a, b = iota((mid, mid), 0), iota((mid, mid), 1)
    same = a % s_loc == b % s_loc
    to_ts = ((b // q_all == a % s_loc) & (b % q_all == a // s_loc)).astype(BF16)
    spread = (iota((q_all, mid), 0) == xor_q(iota((q_all, mid), 1))).astype(BF16)
    second = dot(to_ts, second_factor.reshape(mid, q_all)).astype(BF16)
    second = jnp.where(same, dot(second, spread), 0).astype(BF16)
    to_kqs = ((b // q_all == a % s_loc) & (b % q_all == xor_q(a))).astype(BF16)
    widen = (iota((q_all, mid), 0) == iota((q_all, mid), 1) // s_loc).astype(BF16)
    third = dot(to_kqs, third_factor.reshape(mid, q_all)).astype(BF16)
    third = jnp.where(same, dot(third, widen), 0).astype(BF16)

    kern = kernel.reshape(mid, width).astype(F32)
    gate_vals = gate[0].astype(F32)
    out_grad = cotangent[0].astype(F32)

    def parts_of(x, n):
        size = x.shape[0] // n
        return [x[m * size : (m + 1) * size] for m in range(n)]

    def swap_rows(x):
        return jnp.concatenate(swap_blocks(parts_of(x, nc), "context"), axis=0)

    w_lane = columns_of(weight, lane, nd)
    w_all = jnp.concatenate(gather_blocks(w_lane, "context"), axis=0)
    own_x = jnp.concatenate([columns_of(own, me ^ k, nc) for k in range(nc)], axis=1)
    tokens_all = jnp.concatenate(gather_blocks(own_x, "dp"), axis=0)

    gated = (out_grad * gate_vals).astype(BF16)
    grad_third = dot(fourth, gated).astype(BF16)
    grad_cols = swap_rows(grad_third)
    grad_second = (dot(third, grad_cols, 0, 0) * kern).astype(BF16)
    grad_first = dot(second, grad_second, 0, 0).astype(BF16)
    grad_rows = swap_rows(grad_first)

    proj_lane = dot(tokens_all, w_all).astype(BF16)
    proj = in_order(swap_blocks(parts_of(proj_lane, nd), "dp"), lane, 1)
    first_mix = dot(first, proj).astype(BF16)
    columns_in = swap_rows(first_mix)

    grad_proj = (dot(first, grad_rows, 0, 0) + skip * gated.astype(F32)).astype(BF16)
    grad_lane = jnp.concatenate(
        swap_blocks([columns_of(grad_proj, lane ^ m, nd) for m in range(nd)], "dp"), axis=0
    )

    filtered = (dot(second, columns_in) * kern).astype(BF16)
    third_mix = dot(third, filtered).astype(BF16)
    rows_back = swap_rows(third_mix)

    partial = dot(tokens_all, grad_lane, 0, 0).astype(BF16)
    grad_w = reduce_blocks(parts_of(partial, nc), "context").astype(BF16)
    grad_weight = in_order(gather_blocks(grad_w, "dp"), lane, 1).astype(F32)

    partial = dot(grad_lane, w_all, 1, 1).astype(BF16)
    grad_tokens = reduce_blocks(parts_of(partial, nd), "dp").astype(BF16)
    grad_tokens = jnp.concatenate(
        [columns_of(grad_tokens, me ^ k, nc) for k in range(nc)], axis=1
    )

    pre_gate = dot(fourth, rows_back, 0, 0) + skip * proj.astype(F32)
    mixed = (gate_vals * pre_gate).astype(BF16)
    grad_gate = (out_grad * pre_gate).astype(BF16)
    return (mixed[None], grad_tokens[None], grad_gate[None], grad_weight)


def solution(mesh):
    in_specs = (
        P("dp", "context", None),
        P("context", None),
        P("dp", "context", None),
        P(),
        P("context", None, None),
        P("context", None, None),
        P(None, "context", None),
        P("context", None, None),
        P("context", None, None),
        P("dp", "context", None),
    )
    out_specs = (
        P("dp", "context", None),
        P("dp", "context", None),
        P("dp", "context", None),
        P("context", None),
    )
    return jax.shard_map(
        per_device, mesh=mesh, in_specs=in_specs, out_specs=out_specs, check_vma=False
    )
```

```python
import jax
import jax.numpy as jnp
from jax import lax
from jax.experimental import pallas as pl
from jax.experimental.pallas import tpu as pltpu
from jax.sharding import PartitionSpec as P


BF16 = jnp.bfloat16
F32 = jnp.float32


def dot(a, b, ca=1, cb=0):
    return lax.dot_general(a, b, (((ca,), (cb,)), ((), ())), preferred_element_type=F32)


def bits_of(n):
    return [1 << i for i in range(n.bit_length() - 1)]


def reversed_bits(n):
    order = [0]
    for bit in reversed(bits_of(n)):
        order = order + [m | bit for m in order]
    return order


def exchange(x, axis, bit):
    n = lax.axis_size(axis)
    return lax.ppermute(x, axis, [(i, i ^ bit) for i in range(n)])


def gather_blocks(own, axis):
    have = {0: own}
    for bit in reversed(bits_of(lax.axis_size(axis))):
        have.update({m ^ bit: exchange(x, axis, bit) for m, x in list(have.items())})
    return [have[m] for m in range(len(have))]


def swap_blocks(blocks, axis):
    got = {m: exchange(blocks[m], axis, m) for m in reversed(range(1, len(blocks)))}
    return [blocks[0]] + [got[m] for m in range(1, len(blocks))]


def reduce_halves(keep, give, axis):
    for bit in bits_of(lax.axis_size(axis)):
        got = exchange(give, axis, bit)
        half = keep.shape[0] // 2
        total = lambda a, b: a.astype(F32) + b.astype(F32)
        if half:
            give = total(keep[half:], got[half:]).astype(BF16)
            keep = total(keep[:half], got[:half]).astype(BF16)
    return total(keep, got)[0]


def call(body, outs, args, scratch=(), flops=0, limit=24):
    nbytes = sum(x.size * x.dtype.itemsize for x in (*args, *outs))
    return pl.pallas_call(
        body,
        out_shape=outs,
        in_specs=[pl.BlockSpec(memory_space=pltpu.SMEM)]
        + [pl.BlockSpec(memory_space=pltpu.VMEM)] * (len(args) - 1),
        out_specs=[pl.BlockSpec(memory_space=pltpu.VMEM)] * len(outs),
        scratch_shapes=list(scratch),
        cost_estimate=pl.CostEstimate(flops=flops, bytes_accessed=nbytes, transcendentals=0),
        compiler_params=pltpu.CompilerParams(vmem_limit_bytes=limit << 20),
    )(*args)


def shaped(shape, dtype=BF16):
    return jax.ShapeDtypeStruct(shape, dtype)


def iota(shape, dim):
    return lax.broadcasted_iota(jnp.int32, shape, dim)


def join(refs, columns=slice(None)):
    if refs[0].shape[0] % 16 == 0:
        return jnp.concatenate([r[:, columns] for r in refs], axis=0)
    return jnp.concatenate([r[:, columns].astype(F32) for r in refs], axis=0).astype(BF16)


def window(index, width):
    return pl.ds(pl.multiple_of(index * width, 128), width)


def per_device(
    tokens,
    weight,
    gate,
    skip,
    first_factor,
    second_factor,
    kernel,
    third_factor,
    fourth_factor,
    cotangent,
):
    nc, nd = lax.axis_size("context"), lax.axis_size("dp")
    here = jnp.stack([lax.axis_index("context"), lax.axis_index("dp")]).astype(jnp.int32)
    own = tokens[0]
    rows, width = own.shape
    q_loc, block, _ = first_factor.shape
    s_loc, q_all, _ = second_factor.shape
    part = q_loc * s_loc
    mid = q_all * s_loc
    lane_width = width // nd
    feat = width // nc
    tile = min(width, 512)
    tiles = [slice(i, i + tile) for i in range(0, width, tile)]
    mix_flops = 2 * rows * rows * width
    skip_row = skip.reshape(1, width)
    kern = kernel.reshape(mid, width)
    gate_own, grad_own = gate[0], cotangent[0]

    def diagonal(me, factor_ref, contract):
        row = iota((rows, block), 0)
        source = (me ^ (row // part)) * s_loc + row % s_loc
        pick = (source == iota((rows, block), 1)).astype(BF16)
        of_q = (row % part) // s_loc
        return jnp.concatenate(
            [
                jnp.where(of_q == q, dot(pick, factor_ref[q], 1, contract), 0.0)
                for q in range(q_loc)
            ],
            axis=1,
        ).astype(BF16)

    def put_blocks(refs, value, columns=slice(None)):
        for k, ref in enumerate(refs):
            ref[:, columns] = value[k * part : (k + 1) * part].astype(BF16)

    def lane_body(here_ref, w_ref, out_ref):
        out_ref[...] = w_ref[:, window(here_ref[1], lane_width)]

    (w_lane,) = call(lane_body, [shaped((feat, lane_width))], (here, weight))
    w_blocks = gather_blocks(w_lane, "context")
    token_blocks = gather_blocks(own, "dp")

    def gated_body(here_ref, gate_ref, grad_ref, factor_ref, gated_ref, fourth_ref, *out):
        fourth = diagonal(here_ref[0], factor_ref, 1)
        fourth_ref[...] = fourth
        for t in tiles:
            gated = (grad_ref[:, t].astype(F32) * gate_ref[:, t].astype(F32)).astype(BF16)
            gated_ref[:, t] = gated
            put_blocks(out, dot(fourth, gated), t)

    send = [shaped((part, width))] * nc
    gated, fourth, *grad_third = call(
        gated_body,
        [shaped((rows, width)), shaped((rows, rows)), *send],
        (here, gate_own, grad_own, fourth_factor),
        flops=mix_flops,
    )
    grad_cols = swap_blocks(grad_third, "context")

    def factor_body(here_ref, one_ref, two_ref, three_ref, first_ref, second_ref, third_ref):
        me = here_ref[0]
        first_ref[...] = diagonal(me, one_ref, 0)

        def xor_q(index):
            return (me ^ (index // part)) * q_loc + (index % part) // s_loc

        a, b = iota((mid, mid), 0), iota((mid, mid), 1)
        same = a % s_loc == b % s_loc
        to_ts = ((b // q_all == a % s_loc) & (b % q_all == a // s_loc)).astype(BF16)
        to_kqs = ((b // q_all == a % s_loc) & (b % q_all == xor_q(a))).astype(BF16)
        spread = (iota((q_all, mid), 0) == xor_q(iota((q_all, mid), 1))).astype(BF16)
        widen = (iota((q_all, mid), 0) == iota((q_all, mid), 1) // s_loc).astype(BF16)
        second = dot(dot(to_ts, two_ref[...]).astype(BF16), spread)
        second_ref[...] = jnp.where(same, second, 0.0).astype(BF16)
        third = dot(dot(to_kqs, three_ref[...]).astype(BF16), widen)
        third_ref[...] = jnp.where(same, third, 0.0).astype(BF16)

    first, second, third = call(
        factor_body,
        [shaped((rows, rows)), shaped((mid, mid)), shaped((mid, mid))],
        (
            here,
            first_factor,
            second_factor.reshape(mid, q_all),
            third_factor.reshape(mid, q_all),
        ),
    )

    def back_body(here_ref, third_ref, second_ref, kern_ref, *refs):
        got, out = refs[:nc], refs[nc:]
        for t in tiles:
            mixed = dot(third_ref[...], join(got, t), 0, 0)
            scaled = (mixed * kern_ref[:, t].astype(F32)).astype(BF16)
            put_blocks(out, dot(second_ref[...], scaled, 0, 0), t)

    def forth_body(here_ref, second_ref, third_ref, kern_ref, *refs):
        got, out = refs[:nc], refs[nc:]
        for t in tiles:
            mixed = dot(second_ref[...], join(got, t))
            scaled = (mixed * kern_ref[:, t].astype(F32)).astype(BF16)
            put_blocks(out, dot(third_ref[...], scaled), t)

    grad_first = call(
        back_body, send, (here, third, second, kern, *grad_cols), flops=2 * mix_flops
    )
    grad_rows = swap_blocks(grad_first, "context")

    def proj_body(here_ref, *refs):
        tok, w, out = refs[:nd], refs[nd : nd + nc], refs[nd + nc : nd + nc + nd]
        for m in range(nd):
            total = jnp.zeros((rows, lane_width), F32)
            for k in range(nc):
                total += dot(tok[m][:, window(here_ref[0] ^ k, feat)], w[k][...])
            out[m][...] = total.astype(BF16)

    lanes = [shaped((rows, lane_width))] * nd
    proj_lane = call(
        proj_body,
        lanes,
        (here, *token_blocks, *w_blocks),
        flops=2 * rows * width * width,
        limit=40,
    )
    proj_blocks = swap_blocks(proj_lane, "dp")

    def first_body(here_ref, first_ref, *refs):
        got, proj_ref, out = refs[:nd], refs[nd], refs[nd + 1 :]
        for m in range(nd):
            t = window(here_ref[1] ^ m, lane_width)
            proj_ref[:, t] = got[m][...]
            put_blocks(out, dot(first_ref[...], got[m][...]), t)

    proj, *first_mix = call(
        first_body,
        [shaped((rows, width)), *send],
        (here, first, *proj_blocks),
        flops=mix_flops,
    )
    columns_in = swap_blocks(first_mix, "context")

    def grad_proj_body(here_ref, first_ref, skip_ref, gated_ref, *refs):
        got, out, held = refs[:nc], refs[nc : nc + nd], refs[nc + nd]
        for t in tiles:
            value = dot(first_ref[...], join(got, t), 0, 0)
            value += skip_ref[:, t] * gated_ref[:, t].astype(F32)
            held[:, t] = value.astype(BF16)
        for m in range(nd):
            out[m][...] = held[:, window(here_ref[1] ^ m, lane_width)]

    grad_proj = call(
        grad_proj_body,
        lanes,
        (here, first, skip_row, gated, *grad_rows),
        scratch=[pltpu.VMEM((rows, width), BF16)],
        flops=mix_flops,
    )
    grad_lane = swap_blocks(grad_proj, "dp")

    third_mix = call(
        forth_body, send, (here, second, third, kern, *columns_in), flops=2 * mix_flops
    )
    rows_back = swap_blocks(third_mix, "context")

    def weight_body(here_ref, *refs):
        tok, grad, halves = refs[:nd], refs[nd : 2 * nd], refs[2 * nd :]
        for i, k in enumerate(reversed_bits(nc)):
            total = jnp.zeros((feat, lane_width), F32)
            for m in range(nd):
                total += dot(tok[m][:, window(here_ref[0] ^ k, feat)], grad[m][...], 0, 0)
            halves[i // (nc // 2)][i % (nc // 2)] = total.astype(BF16)

    halves = call(
        weight_body,
        [shaped((nc // 2, feat, lane_width))] * 2,
        (here, *token_blocks, *grad_lane),
        flops=2 * rows * width * width,
        limit=40,
    )
    grad_w = reduce_halves(*halves, "context").astype(BF16)
    grad_w_blocks = gather_blocks(grad_w, "dp")

    def widen_body(here_ref, *refs):
        for m in range(nd):
            refs[nd][:, window(here_ref[1] ^ m, lane_width)] = refs[m][...].astype(F32)

    (grad_weight,) = call(widen_body, [shaped((feat, width), F32)], (here, *grad_w_blocks))

    def tokens_body(here_ref, *refs):
        grad, w, halves = refs[:nd], refs[nd : nd + nc], refs[nd + nc :]
        for i, m in enumerate(reversed_bits(nd)):
            for k in range(nc):
                halves[i // (nd // 2)][i % (nd // 2), :, window(here_ref[0] ^ k, feat)] = dot(
                    grad[m][...], w[k][...], 1, 1
                ).astype(BF16)

    halves = call(
        tokens_body,
        [shaped((nd // 2, rows, width))] * 2,
        (here, *grad_lane, *w_blocks),
        flops=2 * rows * width * width,
        limit=40,
    )
    grad_tokens = reduce_halves(*halves, "dp").astype(BF16)

    def gate_body(here_ref, fourth_ref, skip_ref, proj_ref, gate_ref, grad_ref, *refs):
        got, mixed_ref, grad_gate_ref = refs[:nc], refs[nc], refs[nc + 1]
        for t in tiles:
            pre_gate = dot(fourth_ref[...], join(got, t), 0, 0)
            pre_gate += skip_ref[:, t] * proj_ref[:, t].astype(F32)
            mixed_ref[:, t] = (gate_ref[:, t].astype(F32) * pre_gate).astype(BF16)
            grad_gate_ref[:, t] = (grad_ref[:, t].astype(F32) * pre_gate).astype(BF16)

    mixed, grad_gate = call(
        gate_body,
        [shaped((rows, width))] * 2,
        (here, fourth, skip_row, proj, gate_own, grad_own, *rows_back),
        flops=mix_flops,
    )
    return (mixed[None], grad_tokens[None], grad_gate[None], grad_weight)


def solution(mesh):
    in_specs = (
        P("dp", "context", None),
        P("context", None),
        P("dp", "context", None),
        P(),
        P("context", None, None),
        P("context", None, None),
        P(None, "context", None),
        P("context", None, None),
        P("context", None, None),
        P("dp", "context", None),
    )
    out_specs = (
        P("dp", "context", None),
        P("dp", "context", None),
        P("dp", "context", None),
        P("context", None),
    )
    return jax.shard_map(
        per_device, mesh=mesh, in_specs=in_specs, out_specs=out_specs, check_vma=False
    )
```

```python
import functools

import jax
import jax.numpy as jnp
from jax import lax
from jax.experimental import pallas as pl
from jax.experimental.pallas import tpu as pltpu
from jax.sharding import PartitionSpec as P


BF16 = jnp.bfloat16
F32 = jnp.float32


def dot(a, b, ca=1, cb=0):
    return lax.dot_general(a, b, (((ca,), (cb,)), ((), ())), preferred_element_type=F32)


def bits_of(n):
    return [1 << i for i in range(n.bit_length() - 1)]


def halving_order(bits):
    order = [0]
    for bit in reversed(bits):
        order = order + [m | bit for m in order]
    return order


def two_ways(n):
    bits = bits_of(n)
    return bits, [bits[1], bits[0], *bits[2:]] if n > 2 else bits


def exchange(x, axis, bit):
    n = lax.axis_size(axis)
    return lax.ppermute(x, axis, [(i, i ^ bit) for i in range(n)])


def gather_blocks(own, axis):
    have = {0: own}
    for bit in reversed(bits_of(lax.axis_size(axis))):
        have.update({m ^ bit: exchange(x, axis, bit) for m, x in list(have.items())})
    return [have[m] for m in range(len(have))]


def swap_blocks(blocks, axis):
    return [blocks[0]] + [exchange(blocks[m], axis, m) for m in range(1, len(blocks))]


def add_body(count, last, refs):
    keep, got, out = refs[:count], refs[count : 2 * count], refs[2 * count :]
    for j in range(count):
        for i in range(keep[j].shape[0]):
            total = keep[j][i].astype(F32) + got[j][i].astype(F32)
            if last:
                width = total.shape[1]
                out[0][:, j * width : (j + 1) * width] = total.astype(BF16)
            else:
                half = keep[j].shape[0] // 2
                out[j + (i // half) * count][i % half] = total.astype(BF16)


def reduce_halves(here, keeps, gives, axis, sequences):
    count = len(keeps)
    for bits in zip(*sequences):
        got = [exchange(give, axis, bit) for bit, give in zip(bits, gives)]
        n, rows, width = keeps[0].shape
        last = n == 1
        outs = (
            [shaped((rows, width * count))]
            if last
            else [shaped((n // 2, rows, width))] * (2 * count)
        )
        body = functools.partial(add_body, count, last)
        sums = call(lambda _, *refs, body=body: body(refs), outs, (here, *keeps, *got))
        keeps, gives = sums[:count], sums[count:]
    return keeps[0]


def call(body, outs, args, scratch=(), flops=0, limit=24, in_hbm=()):
    nbytes = sum(x.size * x.dtype.itemsize for x in (*args, *outs))
    return pl.pallas_call(
        body,
        out_shape=outs,
        in_specs=[pl.BlockSpec(memory_space=pltpu.SMEM)]
        + [
            pl.BlockSpec(memory_space=pltpu.HBM if i in in_hbm else pltpu.VMEM)
            for i in range(1, len(args))
        ],
        out_specs=[pl.BlockSpec(memory_space=pltpu.VMEM)] * len(outs),
        scratch_shapes=list(scratch),
        cost_estimate=pl.CostEstimate(flops=flops, bytes_accessed=nbytes, transcendentals=0),
        compiler_params=pltpu.CompilerParams(vmem_limit_bytes=limit << 20),
    )(*args)


def shaped(shape, dtype=BF16):
    return jax.ShapeDtypeStruct(shape, dtype)


def iota(shape, dim):
    return lax.broadcasted_iota(jnp.int32, shape, dim)


def join(refs, columns=slice(None)):
    if refs[0].shape[0] % 16 == 0:
        return jnp.concatenate([r[:, columns] for r in refs], axis=0)
    return jnp.concatenate([r[:, columns].astype(F32) for r in refs], axis=0).astype(BF16)


def window(index, width):
    return pl.ds(pl.multiple_of(index * width, 128), width)


def per_device(
    tokens,
    weight,
    gate,
    skip,
    first_factor,
    second_factor,
    kernel,
    third_factor,
    fourth_factor,
    cotangent,
):
    nc, nd = lax.axis_size("context"), lax.axis_size("dp")
    here = jnp.stack([lax.axis_index("context"), lax.axis_index("dp")]).astype(jnp.int32)
    own = tokens[0]
    rows, width = own.shape
    q_loc, block, _ = first_factor.shape
    s_loc, q_all, _ = second_factor.shape
    part = q_loc * s_loc
    mid = q_all * s_loc
    lane_width = width // nd
    feat = width // nc
    tile = min(width, 512)
    tiles = [slice(i, i + tile) for i in range(0, width, tile)]
    mix_flops = 2 * rows * rows * width
    skip_row = skip.reshape(1, width)
    kern = kernel.reshape(mid, width)
    gate_own, grad_own = gate[0], cotangent[0]

    def diagonal(me, factor_ref, contract):
        row = iota((rows, block), 0)
        source = (me ^ (row // part)) * s_loc + row % s_loc
        pick = (source == iota((rows, block), 1)).astype(BF16)
        of_q = (row % part) // s_loc
        return jnp.concatenate(
            [
                jnp.where(of_q == q, dot(pick, factor_ref[q], 1, contract), 0.0)
                for q in range(q_loc)
            ],
            axis=1,
        ).astype(BF16)

    def put_blocks(refs, value, columns=slice(None)):
        for k, ref in enumerate(refs):
            ref[:, columns] = value[k * part : (k + 1) * part].astype(BF16)

    def lane_body(here_ref, w_ref, out_ref):
        out_ref[...] = w_ref[:, window(here_ref[1], lane_width)]

    (w_lane,) = call(lane_body, [shaped((feat, lane_width))], (here, weight))
    w_blocks = gather_blocks(w_lane, "context")
    token_blocks = gather_blocks(own, "dp")

    def gated_body(here_ref, gate_hbm, grad_hbm, factor_ref, gated_ref, fourth_ref, *refs):
        out, (gate_ref, grad_ref, sems) = refs[:nc], refs[nc:]
        copies = [
            [
                pltpu.make_async_copy(hbm.at[:, t], ref.at[:, t], sems.at[j, i])
                for j, (hbm, ref) in enumerate(((gate_hbm, gate_ref), (grad_hbm, grad_ref)))
            ]
            for i, t in enumerate(tiles)
        ]
        for copy in sum(copies, []):
            copy.start()
        fourth = diagonal(here_ref[0], factor_ref, 1)
        fourth_ref[...] = fourth
        for t, pair in zip(tiles, copies):
            for copy in pair:
                copy.wait()
            gated = (grad_ref[:, t].astype(F32) * gate_ref[:, t].astype(F32)).astype(BF16)
            gated_ref[:, t] = gated
            put_blocks(out, dot(fourth, gated), t)

    send = [shaped((part, width))] * nc
    gated, fourth, *grad_third = call(
        gated_body,
        [shaped((rows, width)), shaped((rows, rows)), *send],
        (here, gate_own, grad_own, fourth_factor),
        scratch=[pltpu.VMEM((rows, width), BF16)] * 2
        + [pltpu.SemaphoreType.DMA((2, len(tiles)))],
        in_hbm=(1, 2),
        flops=mix_flops,
    )
    grad_cols = swap_blocks(grad_third, "context")

    def factor_body(here_ref, one_ref, two_ref, three_ref, first_ref, second_ref, third_ref):
        me = here_ref[0]
        first_ref[...] = diagonal(me, one_ref, 0)

        def xor_q(index):
            return (me ^ (index // part)) * q_loc + (index % part) // s_loc

        a, b = iota((mid, mid), 0), iota((mid, mid), 1)
        same = a % s_loc == b % s_loc
        to_ts = ((b // q_all == a % s_loc) & (b % q_all == a // s_loc)).astype(BF16)
        to_kqs = ((b // q_all == a % s_loc) & (b % q_all == xor_q(a))).astype(BF16)
        spread = (iota((q_all, mid), 0) == xor_q(iota((q_all, mid), 1))).astype(BF16)
        widen = (iota((q_all, mid), 0) == iota((q_all, mid), 1) // s_loc).astype(BF16)
        second = dot(dot(to_ts, two_ref[...]).astype(BF16), spread)
        second_ref[...] = jnp.where(same, second, 0.0).astype(BF16)
        third = dot(dot(to_kqs, three_ref[...]).astype(BF16), widen)
        third_ref[...] = jnp.where(same, third, 0.0).astype(BF16)

    first, second, third = call(
        factor_body,
        [shaped((rows, rows)), shaped((mid, mid)), shaped((mid, mid))],
        (
            here,
            first_factor,
            second_factor.reshape(mid, q_all),
            third_factor.reshape(mid, q_all),
        ),
    )

    def back_body(here_ref, third_ref, second_ref, kern_ref, *refs):
        got, out = refs[:nc], refs[nc:]
        for t in tiles:
            mixed = dot(third_ref[...], join(got, t), 0, 0)
            scaled = (mixed * kern_ref[:, t].astype(F32)).astype(BF16)
            put_blocks(out, dot(second_ref[...], scaled, 0, 0), t)

    def forth_body(here_ref, second_ref, third_ref, kern_ref, *refs):
        got, out = refs[:nc], refs[nc:]
        for t in tiles:
            mixed = dot(second_ref[...], join(got, t))
            scaled = (mixed * kern_ref[:, t].astype(F32)).astype(BF16)
            put_blocks(out, dot(third_ref[...], scaled), t)

    grad_first = call(back_body, send, (here, third, second, kern, *grad_cols), flops=2 * mix_flops)
    grad_rows = swap_blocks(grad_first, "context")

    def proj_body(here_ref, *refs):
        tok, w, out = refs[:nd], refs[nd : nd + nc], refs[nd + nc : nd + nc + nd]
        for m in range(nd):
            total = jnp.zeros((rows, lane_width), F32)
            for k in range(nc):
                total += dot(tok[m][:, window(here_ref[0] ^ k, feat)], w[k][...])
            out[m][...] = total.astype(BF16)

    lanes = [shaped((rows, lane_width))] * nd
    proj_lane = call(
        proj_body, lanes, (here, *token_blocks, *w_blocks), flops=2 * rows * width * width, limit=40
    )
    proj_blocks = swap_blocks(proj_lane, "dp")

    def first_body(here_ref, first_ref, *refs):
        got, proj_ref, out = refs[:nd], refs[nd], refs[nd + 1 :]
        for m in range(nd):
            t = window(here_ref[1] ^ m, lane_width)
            proj_ref[:, t] = got[m][...]
            put_blocks(out, dot(first_ref[...], got[m][...]), t)

    proj, *first_mix = call(
        first_body, [shaped((rows, width)), *send], (here, first, *proj_blocks), flops=mix_flops
    )
    columns_in = swap_blocks(first_mix, "context")

    def grad_proj_body(here_ref, first_ref, skip_ref, gated_ref, *refs):
        got, out, held = refs[:nc], refs[nc : nc + nd], refs[nc + nd]
        for t in tiles:
            value = dot(first_ref[...], join(got, t), 0, 0)
            value += skip_ref[:, t] * gated_ref[:, t].astype(F32)
            held[:, t] = value.astype(BF16)
        for m in range(nd):
            out[m][...] = held[:, window(here_ref[1] ^ m, lane_width)]

    grad_proj = call(
        grad_proj_body,
        lanes,
        (here, first, skip_row, gated, *grad_rows),
        scratch=[pltpu.VMEM((rows, width), BF16)],
        flops=mix_flops,
    )
    grad_lane = swap_blocks(grad_proj, "dp")

    third_mix = call(
        forth_body, send, (here, second, third, kern, *columns_in), flops=2 * mix_flops
    )
    rows_back = swap_blocks(third_mix, "context")

    ways = two_ways(nc)
    half = lane_width // 2

    def weight_body(here_ref, *refs):
        tok, grad, out = refs[:nd], refs[nd : 2 * nd], refs[2 * nd :]
        for k in range(nc):
            total = jnp.zeros((feat, lane_width), F32)
            for m in range(nd):
                total += dot(tok[m][:, window(here_ref[0] ^ k, feat)], grad[m][...], 0, 0)
            for j, bits in enumerate(ways):
                i = halving_order(bits).index(k)
                give, at = divmod(i, nc // 2)
                out[2 * give + j][at] = total[:, j * half : (j + 1) * half].astype(BF16)

    sums = call(
        weight_body,
        [shaped((nc // 2, feat, half))] * 4,
        (here, *token_blocks, *grad_lane),
        flops=2 * rows * width * width,
        limit=40,
    )
    grad_w = reduce_halves(here, sums[:2], sums[2:], "context", ways)
    grad_w_blocks = gather_blocks(grad_w, "dp")

    def widen_body(here_ref, *refs):
        for m in range(nd):
            refs[nd][:, window(here_ref[1] ^ m, lane_width)] = refs[m][...].astype(F32)

    (grad_weight,) = call(widen_body, [shaped((feat, width), F32)], (here, *grad_w_blocks))

    def tokens_body(here_ref, *refs):
        grad, w, halves = refs[:nd], refs[nd : nd + nc], refs[nd + nc :]
        for i, m in enumerate(halving_order(bits_of(nd))):
            for k in range(nc):
                halves[i // (nd // 2)][i % (nd // 2), :, window(here_ref[0] ^ k, feat)] = dot(
                    grad[m][...], w[k][...], 1, 1
                ).astype(BF16)

    halves = call(
        tokens_body,
        [shaped((nd // 2, rows, width))] * 2,
        (here, *grad_lane, *w_blocks),
        flops=2 * rows * width * width,
        limit=40,
    )
    grad_tokens = reduce_halves(here, halves[:1], halves[1:], "dp", [bits_of(nd)])

    def gate_body(here_ref, fourth_ref, skip_ref, proj_ref, gate_ref, grad_ref, *refs):
        got, mixed_ref, grad_gate_ref = refs[:nc], refs[nc], refs[nc + 1]
        for t in tiles:
            pre_gate = dot(fourth_ref[...], join(got, t), 0, 0)
            pre_gate += skip_ref[:, t] * proj_ref[:, t].astype(F32)
            mixed_ref[:, t] = (gate_ref[:, t].astype(F32) * pre_gate).astype(BF16)
            grad_gate_ref[:, t] = (grad_ref[:, t].astype(F32) * pre_gate).astype(BF16)

    mixed, grad_gate = call(
        gate_body,
        [shaped((rows, width))] * 2,
        (here, fourth, skip_row, proj, gate_own, grad_own, *rows_back),
        flops=mix_flops,
    )
    return (mixed[None], grad_tokens[None], grad_gate[None], grad_weight)


def solution(mesh):
    in_specs = (
        P("dp", "context", None),
        P("context", None),
        P("dp", "context", None),
        P(),
        P("context", None, None),
        P("context", None, None),
        P(None, "context", None),
        P("context", None, None),
        P("context", None, None),
        P("dp", "context", None),
    )
    out_specs = (
        P("dp", "context", None),
        P("dp", "context", None),
        P("dp", "context", None),
        P("context", None),
    )

    return jax.shard_map(
        per_device, mesh=mesh, in_specs=in_specs, out_specs=out_specs, check_vma=False
    )
```
